32 devices in a mesh: gx: 8 (over y, x, core), gy: 4 (over z).
Axes of the slice: x: 2, y: 2, z: 4, core: 2. Of those that a mesh axis runs over, the one named last changes fastest.
Arguments:
- block_input: bfloat16 [25088, 512], P(('gx', 'gy')), may hold values from -6 to 6
- cotangent: bfloat16 [25088, 512], P(('gx', 'gy')), may hold values from -6 to 6
- live_images: int32 [8], P('gx'), may hold values from 1 to 16, 96 in all
- ln1_gain: bfloat16 [512], replicated, may hold values from 0.25 to 1.75
- ln1_bias: bfloat16 [512], replicated, may hold values from -3 to 3
- qkv_weight: bfloat16 [512, 3, 512], P('gx', None, 'gy'), may hold values from -0.25 to 0.25
- qv_bias: bfloat16 [2, 512], P(None, 'gy'), may hold values from -3 to 3
- rel_table: bfloat16 [169, 16], P(None, 'gy'), may hold values from -4 to 254
- proj_weight: bfloat16 [512, 512], P('gy', 'gx'), may hold values from -0.75 to 0.75
- proj_bias: bfloat16 [512], replicated, may hold values from -3 to 3
- ln2_gain: bfloat16 [512], replicated, may hold values from 0.25 to 1.75
- ln2_bias: bfloat16 [512], replicated, may hold values from -3 to 3
- fc1_weight: bfloat16 [512, 2048], P('gx', 'gy'), may hold values from -0.25 to 0.25
- fc1_bias: bfloat16 [2048], P('gy'), may hold values from -3 to 3
- fc2_weight: bfloat16 [2048, 512], P('gy', 'gx'), may hold values from -0.1875 to 0.1875
- fc2_bias: bfloat16 [512], replicated, may hold values from -3 to 3
Outputs:
- output: bfloat16 [25088, 512], P(('gx', 'gy'))
- d_input: bfloat16 [25088, 512], P(('gx', 'gy'))
- d_ln1_gain: float32 [512], replicated
- d_ln1_bias: float32 [512], replicated
- d_qkv_weight: float32 [512, 3, 512], P('gx', None, 'gy')
- d_qv_bias: float32 [2, 512], P(None, 'gy')
- d_rel_table: float32 [169, 16], P(None, 'gy')
- d_proj_weight: float32 [512, 512], P('gy', 'gx')
- d_proj_bias: float32 [512], replicated
- d_ln2_gain: float32 [512], replicated
- d_ln2_bias: float32 [512], replicated
- d_fc1_weight: float32 [512, 2048], P('gx', 'gy')
- d_fc1_bias: float32 [2048], P('gy')
- d_fc2_weight: float32 [2048, 512], P('gy', 'gx')
- d_fc2_bias: float32 [512], replicated
The draws below stay inside these ranges and needn't reach their ends.
Inputs may be any that keep to these rules, and one draw needn't show every extreme that they name: Image slot s of index i of gx (slots 0 to 15 in order) holds an image exactly when s < live_images[i]; the counts add up to 96.
All inputs are finite; a program needn't handle non-finite values. No bound on the sum of `live_images` on one device may be relied on, other than what follows from the above.
Results may differ from the reference program's by a relative error of at most 0.014.
Values may be sent and summed in bfloat16 or wider, within the bound.
A program may use at most 192 MiB of HBM per device.

```python
import math
import jax
import jax.numpy as jnp
import numpy as np
from jax import lax

C = 512
H = 16
HD = 32
FF = 2048
GRID = 14
WIN = 7
SHIFT = 3
IMG_DEV = 16
TOKENS = 25088
LIVE = 96
RELS = 169
N_GX = 8


def draw_rel_table(key, part):
    key_base = jax.random.fold_in(key, 0)
    drawn = jnp.clip(jax.random.normal(key_base, (RELS, H), jnp.float32), -3.5, 3.5)
    return drawn.astype(jnp.bfloat16)


def shard_levels(own_key, dims, pieces, low, largest):
    def one(position, shards_of):
        draws = jax.random.uniform(jax.random.fold_in(jax.random.fold_in(own_key, 6), position), (shards_of,), jnp.float32, low / len(pieces), largest / len(pieces))
        return jnp.repeat(jnp.exp(draws), dims[position] // shards_of).reshape((-1,) + (1,) * (len(dims) - position - 1))

    loudness = one(*pieces[0])
    for cut in pieces[1:]:
        loudness = loudness * one(*cut)
    return loudness


def profile(count, total, most, skew):
    loads = [(1 << 20) // math.isqrt(rank ** skew) + 1 for rank in range(2, count + 1)]
    rest, holding = total - most - (count - 1), [1] * (count - 1)
    while rest > 0:
        free = [i for i in range(count - 1) if holding[i] < most]
        mass, left = sum([loads[i] for i in free]), rest
        for i in free:
            addition = min(most - holding[i], max(1, left * loads[i] // mass), rest)
            holding[i] = holding[i] + addition
            rest = rest - addition
    return np.array([most] + holding)


def uneven_parts(stream_key, count, total, bound, lean):
    if count == 2:
        one = jax.random.randint(stream_key, (), max(1, total - bound), min(bound, total - 1) + 1)
        return jnp.stack([one, total - one])
    sizes = jnp.asarray(profile(count, total, bound, lean), jnp.int32)
    pairs = (count - 1) // 2
    giver, taker = sizes[1:1 + 2 * pairs:2], sizes[2:2 + 2 * pairs:2]
    slack = jnp.minimum(giver - 1, bound - taker)
    moved = jax.random.randint(jax.random.fold_in(stream_key, 1), (pairs,), 0, 1 << 20) % (slack + 1)
    sizes = sizes.at[1:1 + 2 * pairs:2].set(giver - moved).at[2:2 + 2 * pairs:2].set(taker + moved)
    return sizes[jax.random.permutation(jax.random.fold_in(stream_key, 2), count)]


def noise(rng, dims, width, bound, cuts=(), kind=jnp.bfloat16):
    result = jax.random.normal(rng, dims, jnp.float32) * width
    if len(cuts) > 0:
        result = shard_levels(rng, dims, cuts, -0.22, 0.18) * result
    return jnp.clip(result, min=-bound, max=bound).astype(kind)


def setup_inputs(seed: int = 0) -> dict:
    key_list = jax.random.split(jax.random.key(seed), 17)
    return {
        "block_input": noise(key_list[0], (TOKENS, C), 1.0, 6.0, ((0, 32),)),
        "cotangent": noise(key_list[1], (TOKENS, C), 1.0, 6.0, ((0, 32),)),
        "live_images": uneven_parts(key_list[2], N_GX, LIVE, IMG_DEV, 1).astype(jnp.int32),
        "ln1_gain": jnp.clip(1.0 + 0.15 * jax.random.normal(key_list[3], (C,), jnp.float32), 0.25, 1.75).astype(jnp.bfloat16),
        "ln1_bias": noise(key_list[4], (C,), 0.5, 3.0),
        "qkv_weight": noise(key_list[5], (C, 3, C), C ** -0.5, 0.25, ((0, 8), (2, 4))),
        "qv_bias": noise(key_list[6], (2, C), 0.5, 3.0, ((1, 4),)),
        "rel_table": draw_rel_table(jax.random.fold_in(key_list[16], 71), 0),
        "proj_weight": noise(key_list[8], (C, C), (C // 7) ** -0.5, 0.75, ((0, 4), (1, 8))),
        "proj_bias": noise(key_list[9], (C,), 0.5, 3.0),
        "ln2_gain": jnp.clip(1.0 + 0.15 * jax.random.normal(key_list[10], (C,), jnp.float32), 0.25, 1.75).astype(jnp.bfloat16),
        "ln2_bias": noise(key_list[11], (C,), 0.5, 3.0),
        "fc1_weight": noise(key_list[12], (C, FF), C ** -0.5, 0.25, ((0, 8), (1, 4))),
        "fc1_bias": noise(key_list[13], (FF,), 0.5, 3.0, ((0, 4),)),
        "fc2_weight": noise(key_list[14], (FF, C), (FF // 2) ** -0.5, 0.1875, ((0, 4), (1, 8))),
        "fc2_bias": noise(key_list[15], (C,), 0.5, 3.0),
    }


eps_norm = 1e-05
mask_value = -100.0
inv_root_two = 0.7071067811865476
inv_root_two_pi = 0.3989422804014327

def window_tables():
    win_area = WIN * WIN
    places = jnp.arange(win_area, dtype=jnp.int32)
    in_row = places // WIN
    in_col = places % WIN
    rel_index = (in_row[:, None] - in_row[None, :] + WIN - 1) * (2 * WIN - 1) + (in_col[:, None] - in_col[None, :] + WIN - 1)
    onehot = (rel_index[:, :, None] == jnp.arange(RELS, dtype=jnp.int32)[None, None, :]).astype(jnp.float32)
    win_count = GRID // WIN
    cells = jnp.arange(GRID, dtype=jnp.int32)
    region = jnp.where(cells < GRID - WIN, 0, jnp.where(cells < GRID - SHIFT, 1, 2))
    cell_id = region[:, None] * 3 + region[None, :]
    win_id = cell_id.reshape(win_count, WIN, win_count, WIN).transpose(0, 2, 1, 3).reshape(win_count, win_count, win_area)
    shift_mask = jnp.where(win_id[:, :, :, None] == win_id[:, :, None, :], 0.0, mask_value).astype(jnp.float32)
    return (onehot, shift_mask)

def to_windows(values, head_count):
    image_count = values.shape[0] // (GRID * GRID)
    win_count = GRID // WIN
    cells = values.reshape(image_count, GRID, GRID, head_count, HD)
    cells = jnp.roll(cells, (-SHIFT, -SHIFT), axis=(1, 2))
    cells = cells.reshape(image_count, win_count, WIN, win_count, WIN, head_count, HD)
    return cells.transpose(0, 1, 3, 5, 2, 4, 6).reshape(image_count, win_count, win_count, head_count, WIN * WIN, HD)

def from_windows(windows):
    image_count, win_count, win_other, head_count = windows.shape[:4]
    cells = windows.reshape(image_count, win_count, win_other, head_count, WIN, WIN, HD).transpose(0, 1, 4, 2, 5, 3, 6)
    cells = cells.reshape(image_count, GRID, GRID, head_count, HD)
    cells = jnp.roll(cells, (SHIFT, SHIFT), axis=(1, 2))
    return cells.reshape(image_count * GRID * GRID, head_count * HD)

def as_float(values):
    return values.astype(jnp.float32)

def rounded(values):
    return lax.optimization_barrier(values.astype(jnp.bfloat16)).astype(jnp.float32)

def window_scores(query_win, keys_win, table, onehot, shift_mask):
    raw = jnp.einsum('nabhid,nabhjd->nabhij', as_float(query_win), as_float(keys_win)) * HD ** (-0.5)
    bias = jnp.einsum('rh,ijr->hij', table, onehot, precision=lax.Precision.HIGHEST)
    return raw + bias[None, None, None] + shift_mask[None, :, :, None]

def attend_forward(query, keys, values, table, onehot, shift_mask, head_count):
    query_win = to_windows(query, head_count)
    keys_win = to_windows(keys, head_count)
    values_win = to_windows(values, head_count)
    scores = window_scores(query_win, keys_win, table, onehot, shift_mask)
    row_top = lax.optimization_barrier(jnp.max(scores, -1, keepdims=True))
    log_total = row_top + jnp.log(lax.optimization_barrier(jnp.sum(jnp.exp(scores - row_top), -1, keepdims=True)))
    probs = rounded(jnp.exp(scores - log_total))
    context = jnp.einsum('nabhij,nabhjd->nabhid', probs, as_float(values_win))
    return (from_windows(context).astype(jnp.bfloat16), log_total)

def attend_backward(query, keys, values, log_total, d_context, table, onehot, shift_mask, head_count):
    query_win = to_windows(query, head_count)
    keys_win = to_windows(keys, head_count)
    values_win = to_windows(values, head_count)
    scores = window_scores(query_win, keys_win, table, onehot, shift_mask)
    probs = jnp.exp(scores - log_total)
    d_win = as_float(to_windows(d_context, head_count))
    d_probs = jnp.einsum('nabhid,nabhjd->nabhij', d_win, as_float(values_win))
    d_values = jnp.einsum('nabhij,nabhid->nabhjd', rounded(probs), d_win)
    row_dot = lax.optimization_barrier(jnp.sum(probs * d_probs, -1, keepdims=True))
    d_scores = probs * (d_probs - row_dot)
    d_table = jnp.einsum('hij,ijr->rh', lax.optimization_barrier(jnp.sum(d_scores, (0, 1, 2))), onehot, precision=lax.Precision.HIGHEST)
    d_scores_low = rounded(d_scores)
    score_scale = HD ** (-0.5)
    d_query = jnp.einsum('nabhij,nabhjd->nabhid', d_scores_low, as_float(keys_win)) * score_scale
    d_keys = jnp.einsum('nabhij,nabhid->nabhjd', d_scores_low, as_float(query_win)) * score_scale
    return (from_windows(d_query), from_windows(d_keys), from_windows(d_values), d_table)

def layer_norm(rows, gain, shift):
    row_mean = lax.optimization_barrier(jnp.mean(rows, -1, keepdims=True))
    row_var = lax.optimization_barrier(jnp.mean(rows * rows, -1, keepdims=True)) - row_mean * row_mean
    inv_std = lax.rsqrt(row_var + eps_norm)
    normed = (rows - row_mean) * inv_std
    return (normed, inv_std, normed * gain + shift)

def norm_back(d_out, normed, inv_std, gain):
    d_normed = d_out * gain
    return inv_std * (d_normed - lax.optimization_barrier(jnp.mean(d_normed, -1, keepdims=True)) - normed * lax.optimization_barrier(jnp.mean(d_normed * normed, -1, keepdims=True)))

def gelu_parts(pre_act):
    cdf_part = 0.5 * (1.0 + jax.scipy.special.erf(pre_act * inv_root_two))
    return (pre_act * cdf_part, cdf_part + pre_act * jnp.exp(-0.5 * pre_act * pre_act) * inv_root_two_pi)

def matmul(left, right):
    return jnp.dot(left, right, preferred_element_type=jnp.float32)

def block_pass(x_rows, cot_rows, live_rows, params, onehot, shift_mask):
    ln1_gain, ln1_bias, qkv_weight, qv_bias, rel_table, proj_weight, proj_bias, ln2_gain, ln2_bias, fc1_weight, fc1_bias, fc2_weight, fc2_bias = params
    resid = x_rows.astype(jnp.float32)
    normed_one, scale_one, pre_one = layer_norm(resid, ln1_gain.astype(jnp.float32), ln1_bias.astype(jnp.float32))
    hidden_one = pre_one.astype(jnp.bfloat16)
    qkv_flat = qkv_weight.reshape(C, 3 * C)
    mixed = matmul(hidden_one, qkv_flat).reshape(-1, 3, C)
    bias_pair = qv_bias.astype(jnp.float32)
    query = (mixed[:, 0] + bias_pair[0]).astype(jnp.bfloat16)
    keys = mixed[:, 1].astype(jnp.bfloat16)
    values = (mixed[:, 2] + bias_pair[1]).astype(jnp.bfloat16)
    table = rel_table.astype(jnp.float32)
    context, log_total = attend_forward(query, keys, values, table, onehot, shift_mask, H)
    resid_one = resid + matmul(context, proj_weight) + proj_bias.astype(jnp.float32)
    normed_two, scale_two, pre_two = layer_norm(resid_one, ln2_gain.astype(jnp.float32), ln2_bias.astype(jnp.float32))
    hidden_two = pre_two.astype(jnp.bfloat16)
    pre_act = matmul(hidden_two, fc1_weight) + fc1_bias.astype(jnp.float32)
    act_full, slope = gelu_parts(pre_act)
    act_low = act_full.astype(jnp.bfloat16)
    output_rows = (resid_one + matmul(act_low, fc2_weight) + fc2_bias.astype(jnp.float32)).astype(jnp.bfloat16)
    grad_out = jnp.where(live_rows[:, None], cot_rows, jnp.zeros_like(cot_rows))
    grad_float = grad_out.astype(jnp.float32)
    d_fc2_bias = lax.optimization_barrier(jnp.sum(grad_float, 0))
    d_fc2_weight = matmul(act_low.T, grad_out)
    d_pre = matmul(grad_out, fc2_weight.T) * slope
    d_fc1_bias = lax.optimization_barrier(jnp.sum(d_pre, 0))
    d_pre_low = d_pre.astype(jnp.bfloat16)
    d_fc1_weight = matmul(hidden_two.T, d_pre_low)
    d_hidden_two = matmul(d_pre_low, fc1_weight.T)
    d_ln2_gain = lax.optimization_barrier(jnp.sum(d_hidden_two * normed_two, 0))
    d_ln2_bias = lax.optimization_barrier(jnp.sum(d_hidden_two, 0))
    d_resid_one = grad_float + norm_back(d_hidden_two, normed_two, scale_two, ln2_gain.astype(jnp.float32))
    d_proj_bias = lax.optimization_barrier(jnp.sum(d_resid_one, 0))
    d_resid_low = d_resid_one.astype(jnp.bfloat16)
    d_proj_weight = matmul(context.T, d_resid_low)
    d_context = matmul(d_resid_low, proj_weight.T).astype(jnp.bfloat16)
    d_query, d_keys, d_values, d_table = attend_backward(query, keys, values, log_total, d_context, table, onehot, shift_mask, H)
    d_qv_bias = jnp.stack([lax.optimization_barrier(jnp.sum(d_query, 0)), lax.optimization_barrier(jnp.sum(d_values, 0))])
    d_mixed = jnp.stack([d_query, d_keys, d_values], 1).astype(jnp.bfloat16).reshape(-1, 3 * C)
    d_qkv_weight = matmul(hidden_one.T, d_mixed).reshape(C, 3, C)
    d_hidden_one = matmul(d_mixed, qkv_flat.T)
    d_ln1_gain = lax.optimization_barrier(jnp.sum(d_hidden_one * normed_one, 0))
    d_ln1_bias = lax.optimization_barrier(jnp.sum(d_hidden_one, 0))
    d_rows = (d_resid_one + norm_back(d_hidden_one, normed_one, scale_one, ln1_gain.astype(jnp.float32))).astype(jnp.bfloat16)
    grads = (d_ln1_gain, d_ln1_bias, d_qkv_weight, d_qv_bias, d_table, d_proj_weight, d_proj_bias, d_ln2_gain, d_ln2_bias, d_fc1_weight, d_fc1_bias, d_fc2_weight, d_fc2_bias)
    return (output_rows, d_rows, grads)

def add_pair(left, right):
    return left + right

def reference(block_input, cotangent, live_images, ln1_gain, ln1_bias, qkv_weight, qv_bias, rel_table, proj_weight, proj_bias, ln2_gain, ln2_bias, fc1_weight, fc1_bias, fc2_weight, fc2_bias):
    onehot, shift_mask = window_tables()
    params = (ln1_gain, ln1_bias, qkv_weight, qv_bias, rel_table, proj_weight, proj_bias, ln2_gain, ln2_bias, fc1_weight, fc1_bias, fc2_weight, fc2_bias)
    block_tokens = IMG_DEV * GRID * GRID
    slot_index = (jnp.arange(block_tokens, dtype=jnp.int32) // (GRID * GRID)).astype(jnp.int32)
    x_blocks = block_input.reshape(N_GX, block_tokens, C)
    cot_blocks = cotangent.reshape(N_GX, block_tokens, C)

    def step_block(carry, inputs):
        x_rows, cot_rows, count = inputs
        live_rows = slot_index < count
        output_rows, d_rows, grads = block_pass(x_rows, cot_rows, live_rows, params, onehot, shift_mask)
        return (jax.tree.map(add_pair, carry, grads), (output_rows, d_rows))
    zeros = tuple((jnp.zeros(param.shape, jnp.float32) for param in params))
    totals, (outputs, d_inputs) = lax.scan(step_block, zeros, (x_blocks, cot_blocks, live_images.astype(jnp.int32)))
    return (outputs.reshape(TOKENS, C), d_inputs.reshape(TOKENS, C), totals[0], totals[1], totals[2], totals[3], totals[4], totals[5], totals[6], totals[7], totals[8], totals[9], totals[10], totals[11], totals[12])
```

```python
import jax
import jax.numpy as jnp
from jax import lax
import numpy as np
from jax.experimental import pallas as pl
from jax.experimental.pallas import tpu as pltpu
from jax.sharding import PartitionSpec as P

HD = 32
GRID = 14
WIN = 7
SHIFT = 3
RELS = 169


eps_norm = 1e-05
mask_value = -100.0
inv_root_two = 0.7071067811865476
inv_root_two_pi = 0.3989422804014327


def matmul(left, right):
    return jnp.dot(left, right, preferred_element_type=jnp.float32)


def matmul_tn(left, right):
    return lax.dot_general(
        left, right, (((0,), (0,)), ((), ())), preferred_element_type=jnp.float32
    )


def matmul_nt(left, right):
    return lax.dot_general(
        left, right, (((1,), (1,)), ((), ())), preferred_element_type=jnp.float32
    )


SLOT = 64
PACK = 8
WIN_COUNT = (GRID // WIN) ** 2
IMAGE = GRID * GRID
ALIGN = 16
STEP = IMAGE // ALIGN * ALIGN
SPAN = STEP + ALIGN
far_below = -1e30


def static_tables(image_count):
    rows = np.arange(WIN_COUNT * SLOT)
    win, place = rows // SLOT, rows % SLOT
    row = (win // (GRID // WIN) * WIN + place // WIN + SHIFT) % GRID
    col = (win % (GRID // WIN) * WIN + place % WIN + SHIFT) % GRID
    token = np.where(place < WIN * WIN, row * GRID + col, -1)
    offset = np.arange(image_count) * (IMAGE - STEP)
    column = np.where(token[None] >= 0, token[None] + offset[:, None], -1)
    places = np.arange(SLOT)
    live = places < WIN * WIN
    pr, pc = places // WIN, places % WIN
    rel = (pr[None, :] - pr[:, None] + WIN - 1) * (2 * WIN - 1) + pc[None, :] - pc[:, None] + WIN - 1
    rel = np.where(live[:, None] & live[None, :], rel, -1)
    cells = np.arange(GRID)
    region = np.where(cells < GRID - WIN, 0, np.where(cells < GRID - SHIFT, 1, 2))
    shifted_row = (win // (GRID // WIN) * WIN + np.minimum(place // WIN, WIN - 1)).reshape(WIN_COUNT, SLOT)
    shifted_col = (win % (GRID // WIN) * WIN + place % WIN).reshape(WIN_COUNT, SLOT)
    ids = region[shifted_row] * 3 + region[shifted_col]
    mask = np.where(ids[:, :, None] == ids[:, None, :], 0.0, mask_value)
    mask = np.where(live[None, None, :] & live[None, :, None], mask, 0.0)
    mask = np.where(live[None, :, None], mask, far_below)
    return column.astype(np.int32), rel.astype(np.int32), mask.astype(np.float32)


def attention_tables(rel_table, image_count):
    column, rel, mask = static_tables(image_count)
    column = jnp.asarray(column)
    spots = jnp.arange(SPAN, dtype=jnp.int32)
    perm = (column[:, :, None] == spots).astype(jnp.bfloat16)
    perm_t = (column[:, None, :] == spots[:, None]).astype(jnp.bfloat16)
    heads = rel_table.shape[1]
    onehot = (jnp.arange(RELS, dtype=jnp.int32)[:, None] == jnp.asarray(rel.reshape(1, -1))).astype(
        jnp.bfloat16
    )
    bias = lax.dot_general(
        rel_table, onehot, (((0,), (0,)), ((), ())), preferred_element_type=jnp.float32
    )
    bias = bias.reshape(heads // PACK, PACK, SLOT, SLOT).transpose(0, 2, 1, 3)
    bias = bias[None] + jnp.asarray(mask)[:, None, :, None, :]
    bias = bias.reshape(WIN_COUNT, heads // PACK, SLOT, PACK * SLOT)
    owner = np.arange(PACK * SLOT)[:, None] // SLOT == np.arange(PACK * HD)[None, :] // HD
    owner = jnp.asarray(owner.astype(np.float32)).astype(jnp.bfloat16)
    return perm, perm_t, bias, owner, onehot


def spread(rows, owner):
    return jnp.concatenate([rows] * PACK, axis=0) * owner


def gather_heads(full):
    lanes = lax.broadcasted_iota(jnp.int32, (SLOT, PACK * HD), 1) // HD
    total = full[:SLOT]
    for h in range(1, PACK):
        total = jnp.where(lanes == h, full[h * SLOT : (h + 1) * SLOT], total)
    return total


def forward_kernel(qkv_ref, perm_ref, perm_t_ref, bias_ref, owner_ref, context_ref, windows_ref, probs_ref, ctx_ref):
    image = pl.program_id(0)
    width = context_ref.shape[1]
    groups = width // (PACK * HD)
    start = pl.multiple_of(image * STEP, ALIGN)
    windows_ref[0] = matmul(perm_ref[0], qkv_ref[pl.ds(start, SPAN), :]).astype(jnp.bfloat16)
    for w in range(WIN_COUNT):
        rows = slice(w * SLOT, (w + 1) * SLOT)
        for g in range(groups):
            low = g * PACK * HD
            query = windows_ref[0, rows, low : low + PACK * HD]
            keys = windows_ref[0, rows, width + low : width + low + PACK * HD]
            values = windows_ref[0, rows, 2 * width + low : 2 * width + low + PACK * HD]
            scores = matmul_nt(keys, spread(query, owner_ref[...])) * HD ** (-0.5) + bias_ref[w, g]
            raised = jnp.exp(scores - jnp.max(scores, 0, keepdims=True))
            probs = raised * (1.0 / jnp.sum(raised, 0, keepdims=True))
            probs_ref[0, w * groups + g] = probs
            full = matmul_tn(probs.astype(jnp.bfloat16), values)
            ctx_ref[rows, low : low + PACK * HD] = gather_heads(full).astype(jnp.bfloat16)

    @pl.when(image == 0)
    def _():
        context_ref[...] = jnp.zeros_like(context_ref)

    context_ref[pl.ds(start, SPAN), :] += matmul(perm_t_ref[0], ctx_ref[...]).astype(jnp.bfloat16)


def backward_kernel(
    d_context_ref, windows_ref, probs_ref, perm_ref, perm_t_ref, owner_ref,
    d_mixed_ref, d_bias_ref, d_qv_ref, d_ctx_ref, d_win_ref,
):
    image = pl.program_id(0)
    width = d_context_ref.shape[1]
    groups = width // (PACK * HD)
    start = pl.multiple_of(image * STEP, ALIGN)

    @pl.when(image == 0)
    def _():
        d_mixed_ref[...] = jnp.zeros_like(d_mixed_ref)
        d_bias_ref[...] = jnp.zeros_like(d_bias_ref)
        d_qv_ref[...] = jnp.zeros_like(d_qv_ref)

    d_ctx_ref[...] = matmul(perm_ref[0], d_context_ref[pl.ds(start, SPAN), :]).astype(jnp.bfloat16)
    for g in range(groups):
        low = g * PACK * HD
        cols = slice(low, low + PACK * HD)
        d_bias = jnp.zeros((SLOT, PACK * SLOT), jnp.float32)
        d_query_sum = jnp.zeros((1, PACK * HD), jnp.float32)
        d_value_sum = jnp.zeros((1, PACK * HD), jnp.float32)
        for w in range(WIN_COUNT):
            rows = slice(w * SLOT, (w + 1) * SLOT)
            query = windows_ref[0, rows, low : low + PACK * HD]
            keys = windows_ref[0, rows, width + low : width + low + PACK * HD]
            values = windows_ref[0, rows, 2 * width + low : 2 * width + low + PACK * HD]
            probs = probs_ref[0, w * groups + g]
            d_wide = spread(d_ctx_ref[rows, cols], owner_ref[...])
            d_probs = matmul_nt(values, d_wide)
            d_values = matmul(probs.astype(jnp.bfloat16), d_wide)
            d_scores = probs * (d_probs - jnp.sum(probs * d_probs, 0, keepdims=True))
            d_bias = d_bias + d_scores
            d_low = d_scores.astype(jnp.bfloat16)
            d_keys = matmul(d_low, spread(query, owner_ref[...])) * HD ** (-0.5)
            d_query = gather_heads(matmul_tn(d_low, keys)) * HD ** (-0.5)
            d_win_ref[rows, low : low + PACK * HD] = d_query.astype(jnp.bfloat16)
            d_win_ref[rows, width + low : width + low + PACK * HD] = d_keys.astype(jnp.bfloat16)
            d_win_ref[rows, 2 * width + low : 2 * width + low + PACK * HD] = d_values.astype(jnp.bfloat16)
            d_query_sum = d_query_sum + jnp.sum(d_query, 0, keepdims=True)
            d_value_sum = d_value_sum + jnp.sum(d_values, 0, keepdims=True)
        d_bias_ref[g] += d_bias
        d_qv_ref[0:1, cols] += d_query_sum
        d_qv_ref[1:2, cols] += d_value_sum
    d_mixed_ref[pl.ds(start, SPAN), :] += matmul(perm_t_ref[0], d_win_ref[...]).astype(jnp.bfloat16)


def whole(shape):
    return pl.BlockSpec(shape, lambda n: (0,) * len(shape))


def per_image(shape):
    return pl.BlockSpec((1,) + shape, lambda n: (n,) + (0,) * len(shape))


def attend_forward(qkv, tables):
    perm, perm_t, bias, owner, _ = tables
    tok, wide = qkv.shape
    width = wide // 3
    count, spots = perm.shape[:2]
    tiles = WIN_COUNT * width // (PACK * HD)
    return pl.pallas_call(
        forward_kernel,
        grid=(count,),
        in_specs=[whole(qkv.shape), per_image((spots, SPAN)), per_image((SPAN, spots)), whole(bias.shape), whole(owner.shape)],
        out_specs=[whole((tok, width)), per_image((spots, wide)), per_image((tiles, SLOT, PACK * SLOT))],
        out_shape=[
            jax.ShapeDtypeStruct((tok, width), jnp.bfloat16),
            jax.ShapeDtypeStruct((count, spots, wide), jnp.bfloat16),
            jax.ShapeDtypeStruct((count, tiles, SLOT, PACK * SLOT), jnp.float32),
        ],
        scratch_shapes=[pltpu.VMEM((spots, width), jnp.bfloat16)],
        name="attend_forward",
    )(qkv, perm, perm_t, bias, owner)


def attend_backward(d_context, windows, probs, tables):
    perm, perm_t, _, owner, onehot = tables
    tok, width = d_context.shape
    count, spots, wide = windows.shape
    groups = width // (PACK * HD)
    tiles = probs.shape[1]
    d_mixed, d_bias, d_qv = pl.pallas_call(
        backward_kernel,
        grid=(count,),
        in_specs=[
            whole(d_context.shape), per_image((spots, wide)), per_image((tiles, SLOT, PACK * SLOT)),
            per_image((spots, SPAN)), per_image((SPAN, spots)), whole(owner.shape),
        ],
        out_specs=[whole((tok, wide)), whole((groups, SLOT, PACK * SLOT)), whole((2, width))],
        out_shape=[
            jax.ShapeDtypeStruct((tok, wide), jnp.bfloat16),
            jax.ShapeDtypeStruct((groups, SLOT, PACK * SLOT), jnp.float32),
            jax.ShapeDtypeStruct((2, width), jnp.float32),
        ],
        scratch_shapes=[pltpu.VMEM((spots, width), jnp.bfloat16), pltpu.VMEM((spots, wide), jnp.bfloat16)],
        name="attend_backward",
    )(d_context, windows, probs, perm, perm_t, owner)
    d_bias = d_bias.reshape(groups, SLOT, PACK, SLOT).transpose(0, 2, 1, 3).reshape(groups * PACK, SLOT * SLOT)
    d_table = lax.dot_general(
        onehot.astype(jnp.float32), d_bias, (((1,), (1,)), ((), ())), precision=lax.Precision.HIGHEST
    )
    return d_mixed, d_qv, d_table


def gelu_parts(pre_act):
    cdf_part = 0.5 * (1.0 + jax.scipy.special.erf(pre_act * inv_root_two))
    return (
        pre_act * cdf_part,
        cdf_part + pre_act * jnp.exp(-0.5 * pre_act * pre_act) * inv_root_two_pi,
    )


def layer_norm(rows, gain, shift):
    row_mean = jnp.mean(rows, -1, keepdims=True)
    row_var = jnp.mean(rows * rows, -1, keepdims=True) - row_mean * row_mean
    inv_std = lax.rsqrt(row_var + eps_norm)
    normed = (rows - row_mean) * inv_std
    return (normed, inv_std, normed * gain + shift)


def norm_back(d_out, normed, inv_std, gain):
    d_normed = d_out * gain
    return inv_std * (
        d_normed
        - jnp.mean(d_normed, -1, keepdims=True)
        - normed * jnp.mean(d_normed * normed, -1, keepdims=True)
    )


def whole_matrix(block, gx_dim, gy_dim):
    both = lax.all_gather(block, ("gx", "gy"), axis=0, tiled=False)
    gx_size, gy_size = lax.axis_size("gx"), lax.axis_size("gy")
    both = both.reshape((gx_size, gy_size) + block.shape)
    shape = [d for d in block.shape]
    if gx_dim < gy_dim:
        if block.ndim == 3:
            out = both.transpose(0, 2, 3, 1, 4)
        else:
            out = both.transpose(0, 2, 1, 3)
    else:
        out = both.transpose(1, 2, 0, 3)
    shape[gx_dim] *= gx_size
    shape[gy_dim] *= gy_size
    return out.reshape(shape)


def share_matrix(grad, gx_dim, gy_dim):
    gx_size, gy_size = lax.axis_size("gx"), lax.axis_size("gy")
    grad = grad.astype(jnp.bfloat16)
    if grad.ndim == 3:
        a, b, c = grad.shape
        blocks = grad.reshape(gx_size, a // gx_size, b, gy_size, c // gy_size).transpose(0, 3, 1, 2, 4)
    elif gx_dim < gy_dim:
        a, c = grad.shape
        blocks = grad.reshape(gx_size, a // gx_size, gy_size, c // gy_size).transpose(0, 2, 1, 3)
    else:
        a, c = grad.shape
        blocks = grad.reshape(gy_size, a // gy_size, gx_size, c // gx_size).transpose(2, 0, 1, 3)
    blocks = blocks.reshape((gx_size * gy_size,) + blocks.shape[2:])
    mine = lax.psum_scatter(blocks, ("gx", "gy"), scatter_dimension=0, tiled=False)
    return mine.astype(jnp.float32)


def own_columns(summed, axis):
    size = summed.shape[axis] // lax.axis_size("gy")
    return lax.dynamic_slice_in_dim(summed, lax.axis_index("gy") * size, size, axis)


def local_live(tok_local, live_images):
    position = lax.axis_index("gy")
    per_device = tok_local // (GRID * GRID)
    slot_index = position * per_device + jnp.arange(tok_local, dtype=jnp.int32) // (GRID * GRID)
    return slot_index < live_images[0]


def blocked_layer(block_input, cotangent, live_images, params):
    (
        ln1_gain,
        ln1_bias,
        qkv_weight,
        qv_bias,
        rel_table,
        proj_weight,
        proj_bias,
        ln2_gain,
        ln2_bias,
        fc1_weight,
        fc1_bias,
        fc2_weight,
        fc2_bias,
    ) = params
    tok_local, width = block_input.shape
    qkv_rows = whole_matrix(qkv_weight, 0, 2)
    proj_cols = whole_matrix(proj_weight, 1, 0)
    fc1_rows = whole_matrix(fc1_weight, 0, 1)
    fc2_cols = whole_matrix(fc2_weight, 1, 0)
    qv_bias = lax.all_gather(qv_bias, "gy", axis=1, tiled=True)
    rel_table = lax.all_gather(rel_table, "gy", axis=1, tiled=True)
    fc1_bias = lax.all_gather(fc1_bias, "gy", axis=0, tiled=True)
    feat_local = width
    qkv_flat = qkv_rows.reshape(width, 3 * feat_local)
    gain_one = ln1_gain.astype(jnp.float32)
    gain_two = ln2_gain.astype(jnp.float32)
    resid = block_input.astype(jnp.float32)
    normed_one, scale_one, pre_one = layer_norm(resid, gain_one, ln1_bias.astype(jnp.float32))
    hidden_one = (pre_one.astype(jnp.bfloat16))
    bias_row = jnp.stack([qv_bias[0], jnp.zeros_like(qv_bias[0]), qv_bias[1]]).reshape(1, 3 * width)
    mixed = (matmul(hidden_one, qkv_flat) + bias_row.astype(jnp.float32)).astype(jnp.bfloat16)
    tables = attention_tables(rel_table, tok_local // IMAGE)
    context, windows, probs = attend_forward(mixed, tables)
    resid_one = resid + (matmul(context, proj_cols)) + proj_bias.astype(jnp.float32)
    normed_two, scale_two, pre_two = layer_norm(resid_one, gain_two, ln2_bias.astype(jnp.float32))
    hidden_two = (pre_two.astype(jnp.bfloat16))
    pre_act = matmul(hidden_two, fc1_rows) + fc1_bias.astype(jnp.float32)
    act_full, slope = gelu_parts(pre_act)
    act_low = act_full.astype(jnp.bfloat16)
    output = (
        resid_one + (matmul(act_low, fc2_cols)) + fc2_bias.astype(jnp.float32)
    ).astype(jnp.bfloat16)
    live_rows = local_live(tok_local, live_images)
    grad_out = jnp.where(live_rows[:, None], cotangent, jnp.zeros_like(cotangent))
    grad_float = grad_out.astype(jnp.float32)
    grad_full = (grad_out)
    d_fc2_bias = jnp.sum(grad_float, 0)
    d_fc2_weight = matmul_tn(act_low, grad_full)
    d_pre = matmul_nt(grad_full, fc2_cols) * slope
    d_fc1_bias = jnp.sum(d_pre, 0)
    d_pre_low = d_pre.astype(jnp.bfloat16)
    d_fc1_weight = matmul_tn(hidden_two, d_pre_low)
    d_hidden_two = (matmul_nt(d_pre_low, fc1_rows))
    d_ln2_gain = jnp.sum(d_hidden_two * normed_two, 0)
    d_ln2_bias = jnp.sum(d_hidden_two, 0)
    d_resid_one = grad_float + norm_back(d_hidden_two, normed_two, scale_two, gain_two)
    d_proj_bias = jnp.sum(d_resid_one, 0)
    d_resid_full = (d_resid_one.astype(jnp.bfloat16))
    d_proj_weight = matmul_tn(context, d_resid_full)
    d_context = matmul_nt(d_resid_full, proj_cols).astype(jnp.bfloat16)
    d_mixed, d_qv_bias, d_table = attend_backward(d_context, windows, probs, tables)
    d_qkv_weight = matmul_tn(hidden_one, d_mixed).reshape(width, 3, feat_local)
    d_hidden_one = (matmul_nt(d_mixed, qkv_flat))
    d_ln1_gain = jnp.sum(d_hidden_one * normed_one, 0)
    d_ln1_bias = jnp.sum(d_hidden_one, 0)
    d_input = (d_resid_one + norm_back(d_hidden_one, normed_one, scale_one, gain_one)).astype(
        jnp.bfloat16
    )
    d_fc2_weight = share_matrix(d_fc2_weight, 1, 0)
    d_fc1_weight = share_matrix(d_fc1_weight, 0, 1)
    d_proj_weight = share_matrix(d_proj_weight, 1, 0)
    d_qkv_weight = share_matrix(d_qkv_weight, 0, 2)
    sums = lax.psum(
        (d_ln1_gain, d_ln1_bias, d_proj_bias, d_ln2_gain, d_ln2_bias, d_fc2_bias,
         d_qv_bias, d_table, d_fc1_bias), ("gx", "gy")
    )
    norm_sums = sums[:6]
    head_sums = (own_columns(sums[6], 1), own_columns(sums[7], 1), own_columns(sums[8], 0))
    return (
        output,
        d_input,
        norm_sums[0],
        norm_sums[1],
        d_qkv_weight,
        head_sums[0],
        head_sums[1],
        d_proj_weight,
        norm_sums[2],
        norm_sums[3],
        norm_sums[4],
        d_fc1_weight,
        head_sums[2],
        d_fc2_weight,
        norm_sums[5],
    )


def shards(
    block_input,
    cotangent,
    live_images,
    ln1_gain,
    ln1_bias,
    qkv_weight,
    qv_bias,
    rel_table,
    proj_weight,
    proj_bias,
    ln2_gain,
    ln2_bias,
    fc1_weight,
    fc1_bias,
    fc2_weight,
    fc2_bias,
):
    params = (
        ln1_gain,
        ln1_bias,
        qkv_weight,
        qv_bias,
        rel_table,
        proj_weight,
        proj_bias,
        ln2_gain,
        ln2_bias,
        fc1_weight,
        fc1_bias,
        fc2_weight,
        fc2_bias,
    )
    results = blocked_layer(block_input, cotangent, live_images, params)
    return results


def solution(mesh):
    return jax.shard_map(
        shards,
        mesh=mesh,
        in_specs=(
            P(("gx", "gy"), None),
            P(("gx", "gy"), None),
            P("gx"),
            P(),
            P(),
            P("gx", None, "gy"),
            P(None, "gy"),
            P(None, "gy"),
            P("gy", "gx"),
            P(),
            P(),
            P(),
            P("gx", "gy"),
            P("gy"),
            P("gy", "gx"),
            P(),
        ),
        out_specs=(
            P(("gx", "gy"), None),
            P(("gx", "gy"), None),
            P(),
            P(),
            P("gx", None, "gy"),
            P(None, "gy"),
            P(None, "gy"),
            P("gy", "gx"),
            P(),
            P(),
            P(),
            P("gx", "gy"),
            P("gy"),
            P("gy", "gx"),
            P(),
        ),
        check_vma=False,
    )
```

```python
import jax
import jax.numpy as jnp
from jax import lax
import numpy as np
from jax.experimental import pallas as pl
from jax.experimental.pallas import tpu as pltpu
from jax.sharding import PartitionSpec as P

HD = 32
GRID = 14
WIN = 7
SHIFT = 3
RELS = 169


eps_norm = 1e-05
mask_value = -100.0
inv_root_two = 0.7071067811865476
inv_root_two_pi = 0.3989422804014327


def matmul(left, right):
    return jnp.dot(left, right, preferred_element_type=jnp.float32)


def matmul_tn(left, right):
    return lax.dot_general(
        left, right, (((0,), (0,)), ((), ())), preferred_element_type=jnp.float32
    )


def matmul_nt(left, right):
    return lax.dot_general(
        left, right, (((1,), (1,)), ((), ())), preferred_element_type=jnp.float32
    )


SLOT = 64
PACK = 8
WIN_COUNT = (GRID // WIN) ** 2
IMAGE = GRID * GRID
ALIGN = 16
STEP = IMAGE // ALIGN * ALIGN
SPAN = STEP + ALIGN
far_below = -1e30


def static_tables(image_count):
    rows = np.arange(WIN_COUNT * SLOT)
    win, place = rows // SLOT, rows % SLOT
    row = (win // (GRID // WIN) * WIN + place // WIN + SHIFT) % GRID
    col = (win % (GRID // WIN) * WIN + place % WIN + SHIFT) % GRID
    token = np.where(place < WIN * WIN, row * GRID + col, -1)
    offset = np.arange(image_count) * (IMAGE - STEP)
    column = np.where(token[None] >= 0, token[None] + offset[:, None], -1)
    places = np.arange(SLOT)
    live = places < WIN * WIN
    pr, pc = places // WIN, places % WIN
    rel = (pr[None, :] - pr[:, None] + WIN - 1) * (2 * WIN - 1) + pc[None, :] - pc[:, None] + WIN - 1
    rel = np.where(live[:, None] & live[None, :], rel, -1)
    cells = np.arange(GRID)
    region = np.where(cells < GRID - WIN, 0, np.where(cells < GRID - SHIFT, 1, 2))
    shifted_row = (win // (GRID // WIN) * WIN + np.minimum(place // WIN, WIN - 1)).reshape(WIN_COUNT, SLOT)
    shifted_col = (win % (GRID // WIN) * WIN + place % WIN).reshape(WIN_COUNT, SLOT)
    ids = region[shifted_row] * 3 + region[shifted_col]
    mask = np.where(ids[:, :, None] == ids[:, None, :], 0.0, mask_value)
    mask = np.where(live[None, None, :] & live[None, :, None], mask, 0.0)
    mask = np.where(live[None, :, None], mask, far_below)
    return column.astype(np.int32), rel.astype(np.int32), mask.astype(np.float32)


def attention_tables(rel_table, image_count):
    column, rel, mask = static_tables(image_count)
    column = jnp.asarray(column)
    spots = jnp.arange(SPAN, dtype=jnp.int32)
    perm = (column[:, :, None] == spots).astype(jnp.bfloat16)
    perm_t = (column[:, None, :] == spots[:, None]).astype(jnp.bfloat16)
    heads = rel_table.shape[1]
    onehot = (jnp.arange(RELS, dtype=jnp.int32)[:, None] == jnp.asarray(rel.reshape(1, -1))).astype(
        jnp.bfloat16
    )
    bias = lax.dot_general(
        rel_table, onehot, (((0,), (0,)), ((), ())), preferred_element_type=jnp.float32
    )
    bias = bias.reshape(heads // PACK, PACK, SLOT, SLOT).transpose(0, 2, 1, 3)
    bias = bias[None] + jnp.asarray(mask)[:, None, :, None, :]
    bias = bias.reshape(WIN_COUNT, heads // PACK, SLOT, PACK * SLOT)
    owner = np.arange(PACK * SLOT)[:, None] // SLOT == np.arange(PACK * HD)[None, :] // HD
    owner = jnp.asarray(owner.astype(np.float32)).astype(jnp.bfloat16)
    return perm, perm_t, bias, owner, onehot


def spread(rows, owner):
    return jnp.concatenate([rows] * PACK, axis=0) * owner


def gather_heads(full):
    lanes = lax.broadcasted_iota(jnp.int32, (SLOT, PACK * HD), 1) // HD
    total = full[:SLOT]
    for h in range(1, PACK):
        total = jnp.where(lanes == h, full[h * SLOT : (h + 1) * SLOT], total)
    return total


def forward_kernel(qkv_ref, perm_ref, perm_t_ref, bias_ref, owner_ref, context_ref, windows_ref, probs_ref, ctx_ref):
    image = pl.program_id(0)
    width = context_ref.shape[1]
    groups = width // (PACK * HD)
    start = pl.multiple_of(image * STEP, ALIGN)
    windows_ref[0] = matmul(perm_ref[0], qkv_ref[pl.ds(start, SPAN), :]).astype(jnp.bfloat16)
    for w in range(WIN_COUNT):
        rows = slice(w * SLOT, (w + 1) * SLOT)
        for g in range(groups):
            low = g * PACK * HD
            query = windows_ref[0, rows, low : low + PACK * HD]
            keys = windows_ref[0, rows, width + low : width + low + PACK * HD]
            values = windows_ref[0, rows, 2 * width + low : 2 * width + low + PACK * HD]
            scores = matmul_nt(keys, spread(query, owner_ref[...])) * HD ** (-0.5) + bias_ref[w, g]
            raised = jnp.exp(scores - jnp.max(scores, 0, keepdims=True))
            probs = raised * (1.0 / jnp.sum(raised, 0, keepdims=True))
            probs_ref[0, w * groups + g] = probs
            full = matmul_tn(probs.astype(jnp.bfloat16), values)
            ctx_ref[rows, low : low + PACK * HD] = gather_heads(full).astype(jnp.bfloat16)

    @pl.when(image == 0)
    def _():
        context_ref[...] = jnp.zeros_like(context_ref)

    context_ref[pl.ds(start, SPAN), :] += matmul(perm_t_ref[0], ctx_ref[...]).astype(jnp.bfloat16)


def backward_kernel(
    d_context_ref, windows_ref, probs_ref, perm_ref, perm_t_ref, owner_ref,
    d_mixed_ref, d_bias_ref, d_qv_ref, d_ctx_ref, d_win_ref,
):
    image = pl.program_id(0)
    width = d_context_ref.shape[1]
    groups = width // (PACK * HD)
    start = pl.multiple_of(image * STEP, ALIGN)

    @pl.when(image == 0)
    def _():
        d_mixed_ref[...] = jnp.zeros_like(d_mixed_ref)
        d_bias_ref[...] = jnp.zeros_like(d_bias_ref)
        d_qv_ref[...] = jnp.zeros_like(d_qv_ref)

    d_ctx_ref[...] = matmul(perm_ref[0], d_context_ref[pl.ds(start, SPAN), :]).astype(jnp.bfloat16)
    for g in range(groups):
        low = g * PACK * HD
        cols = slice(low, low + PACK * HD)
        d_bias = jnp.zeros((SLOT, PACK * SLOT), jnp.float32)
        d_query_sum = jnp.zeros((1, PACK * HD), jnp.float32)
        d_value_sum = jnp.zeros((1, PACK * HD), jnp.float32)
        for w in range(WIN_COUNT):
            rows = slice(w * SLOT, (w + 1) * SLOT)
            query = windows_ref[0, rows, low : low + PACK * HD]
            keys = windows_ref[0, rows, width + low : width + low + PACK * HD]
            values = windows_ref[0, rows, 2 * width + low : 2 * width + low + PACK * HD]
            probs = probs_ref[0, w * groups + g]
            d_wide = spread(d_ctx_ref[rows, cols], owner_ref[...])
            d_probs = matmul_nt(values, d_wide)
            d_values = matmul(probs.astype(jnp.bfloat16), d_wide)
            d_scores = probs * (d_probs - jnp.sum(probs * d_probs, 0, keepdims=True))
            d_bias = d_bias + d_scores
            d_low = d_scores.astype(jnp.bfloat16)
            d_keys = matmul(d_low, spread(query, owner_ref[...])) * HD ** (-0.5)
            d_query = gather_heads(matmul_tn(d_low, keys)) * HD ** (-0.5)
            d_win_ref[rows, low : low + PACK * HD] = d_query.astype(jnp.bfloat16)
            d_win_ref[rows, width + low : width + low + PACK * HD] = d_keys.astype(jnp.bfloat16)
            d_win_ref[rows, 2 * width + low : 2 * width + low + PACK * HD] = d_values.astype(jnp.bfloat16)
            d_query_sum = d_query_sum + jnp.sum(d_query, 0, keepdims=True)
            d_value_sum = d_value_sum + jnp.sum(d_values, 0, keepdims=True)
        d_bias_ref[g] += d_bias
        d_qv_ref[0:1, cols] += d_query_sum
        d_qv_ref[1:2, cols] += d_value_sum
    d_mixed_ref[pl.ds(start, SPAN), :] += matmul(perm_t_ref[0], d_win_ref[...]).astype(jnp.bfloat16)


def whole(shape):
    return pl.BlockSpec(shape, lambda n: (0,) * len(shape))


def per_image(shape):
    return pl.BlockSpec((1,) + shape, lambda n: (n,) + (0,) * len(shape))


def attend_forward(qkv, tables):
    perm, perm_t, bias, owner, _ = tables
    tok, wide = qkv.shape
    width = wide // 3
    count, spots = perm.shape[:2]
    tiles = WIN_COUNT * width // (PACK * HD)
    return pl.pallas_call(
        forward_kernel,
        grid=(count,),
        in_specs=[whole(qkv.shape), per_image((spots, SPAN)), per_image((SPAN, spots)), whole(bias.shape), whole(owner.shape)],
        out_specs=[whole((tok, width)), per_image((spots, wide)), per_image((tiles, SLOT, PACK * SLOT))],
        out_shape=[
            jax.ShapeDtypeStruct((tok, width), jnp.bfloat16),
            jax.ShapeDtypeStruct((count, spots, wide), jnp.bfloat16),
            jax.ShapeDtypeStruct((count, tiles, SLOT, PACK * SLOT), jnp.float32),
        ],
        scratch_shapes=[pltpu.VMEM((spots, width), jnp.bfloat16)],
        name="attend_forward",
    )(qkv, perm, perm_t, bias, owner)


def attend_backward(d_context, windows, probs, tables):
    perm, perm_t, _, owner, onehot = tables
    tok, width = d_context.shape
    count, spots, wide = windows.shape
    groups = width // (PACK * HD)
    tiles = probs.shape[1]
    d_mixed, d_bias, d_qv = pl.pallas_call(
        backward_kernel,
        grid=(count,),
        in_specs=[
            whole(d_context.shape), per_image((spots, wide)), per_image((tiles, SLOT, PACK * SLOT)),
            per_image((spots, SPAN)), per_image((SPAN, spots)), whole(owner.shape),
        ],
        out_specs=[whole((tok, wide)), whole((groups, SLOT, PACK * SLOT)), whole((2, width))],
        out_shape=[
            jax.ShapeDtypeStruct((tok, wide), jnp.bfloat16),
            jax.ShapeDtypeStruct((groups, SLOT, PACK * SLOT), jnp.float32),
            jax.ShapeDtypeStruct((2, width), jnp.float32),
        ],
        scratch_shapes=[pltpu.VMEM((spots, width), jnp.bfloat16), pltpu.VMEM((spots, wide), jnp.bfloat16)],
        name="attend_backward",
    )(d_context, windows, probs, perm, perm_t, owner)
    d_bias = d_bias.reshape(groups, SLOT, PACK, SLOT).transpose(0, 2, 1, 3).reshape(groups * PACK, SLOT * SLOT)
    d_table = lax.dot_general(
        onehot.astype(jnp.float32), d_bias, (((1,), (1,)), ((), ())), precision=lax.Precision.HIGHEST
    )
    return d_mixed, d_qv, d_table


def gelu_parts(pre_act):
    cdf_part = 0.5 * (1.0 + jax.scipy.special.erf(pre_act * inv_root_two))
    return (
        pre_act * cdf_part,
        cdf_part + pre_act * jnp.exp(-0.5 * pre_act * pre_act) * inv_root_two_pi,
    )


def layer_norm(rows, gain, shift):
    row_mean = jnp.mean(rows, -1, keepdims=True)
    row_var = jnp.mean(rows * rows, -1, keepdims=True) - row_mean * row_mean
    inv_std = lax.rsqrt(row_var + eps_norm)
    normed = (rows - row_mean) * inv_std
    return (normed, inv_std, normed * gain + shift)


def norm_back(d_out, normed, inv_std, gain):
    d_normed = d_out * gain
    return inv_std * (
        d_normed
        - jnp.mean(d_normed, -1, keepdims=True)
        - normed * jnp.mean(d_normed * normed, -1, keepdims=True)
    )


def axis_bits(name):
    return lax.axis_size(name).bit_length() - 1


def exchange(value, name, bit):
    pairs = [(i, i ^ (1 << bit)) for i in range(lax.axis_size(name))]
    return lax.ppermute(value, name, pairs)


def own_bit(name, bit):
    return (lax.axis_index(name) >> bit) & 1


def gather_order(name, flip):
    bits = list(range(axis_bits(name)))[::-1]
    if flip and len(bits) > 2:
        bits = [bits[1], bits[0]] + bits[2:]
    return bits


def gather_axis(block, name, flip=False):
    rows, columns = block.shape
    done = []
    for bit in gather_order(name, flip):
        higher = 1 << len([b for b in done if b > bit])
        lower = 1 << len([b for b in done if b < bit])
        mine = block.reshape(higher, 1, lower * rows, columns)
        theirs = exchange(block, name, bit).reshape(mine.shape)
        upper = own_bit(name, bit) == 1
        block = jnp.concatenate(
            [jnp.where(upper, theirs, mine), jnp.where(upper, mine, theirs)], axis=1
        ).reshape(higher * 2 * lower * rows, columns)
        done.append(bit)
    return block


def scatter_axis(total, name, flip=False):
    columns = total.shape[1]
    rows = total.shape[0] // lax.axis_size(name)
    order = gather_order(name, flip)[::-1]
    for place, bit in enumerate(order):
        left = order[place + 1 :]
        higher = 1 << len([b for b in left if b > bit])
        lower = 1 << len([b for b in left if b < bit])
        view = total.reshape(higher, 2, lower * rows, columns)
        mine = own_bit(name, bit)
        away = lax.dynamic_index_in_dim(view, 1 - mine, 1, keepdims=False).astype(jnp.bfloat16)
        kept = lax.dynamic_index_in_dim(view, mine, 1, keepdims=False)
        total = (kept + exchange(away, name, bit).astype(jnp.float32)).reshape(-1, columns)
    return total


def sum_all(value):
    for name in ("gx", "gy"):
        for bit in range(axis_bits(name)):
            value = value + exchange(value, name, bit)
    return value


def whole_matrix(block, groups, flip):
    rows, columns = block.shape[0], block.shape[1] // groups
    gy_size = lax.axis_size("gy")
    block = gather_axis(block, "gy").reshape(gy_size, rows, groups, columns)
    block = block.transpose(1, 2, 0, 3).reshape(rows, groups * gy_size * columns)
    return gather_axis(block, "gx", flip)


def share_matrix(grad, groups, flip):
    gy_size = lax.axis_size("gy")
    mine = scatter_axis(grad, "gx", flip)
    rows, columns = mine.shape[0], mine.shape[1] // groups // gy_size
    mine = mine.reshape(rows, groups, gy_size, columns).transpose(2, 0, 1, 3)
    return scatter_axis(mine.reshape(gy_size * rows, groups * columns), "gy")


def pack(values):
    flat = [value.reshape(-1) for value in values]
    size = sum(value.shape[0] for value in flat)
    return jnp.pad(jnp.concatenate(flat), (0, -size % 2048)).reshape(-1, 128)


def unpack(packed, shapes):
    flat, at, out = packed.reshape(-1), 0, []
    for shape in shapes:
        size = int(np.prod(shape))
        out.append(flat[at : at + size].reshape(shape))
        at += size
    return out


def own_columns(summed, axis):
    size = summed.shape[axis] // lax.axis_size("gy")
    return lax.dynamic_slice_in_dim(summed, lax.axis_index("gy") * size, size, axis)


def local_live(tok_local, live_images):
    position = lax.axis_index("gy")
    per_device = tok_local // (GRID * GRID)
    slot_index = position * per_device + jnp.arange(tok_local, dtype=jnp.int32) // (GRID * GRID)
    return slot_index < live_images[0]


def blocked_layer(block_input, cotangent, live_images, params):
    (
        ln1_gain,
        ln1_bias,
        qkv_weight,
        qv_bias,
        rel_table,
        proj_weight,
        proj_bias,
        ln2_gain,
        ln2_bias,
        fc1_weight,
        fc1_bias,
        fc2_weight,
        fc2_bias,
    ) = params
    tok_local, width = block_input.shape
    gy_size = lax.axis_size("gy")
    small = pack((qv_bias, rel_table, fc1_bias))
    small_rows = small.shape[0]
    small = gather_axis(small, "gy")
    parts = [
        unpack(small[i * small_rows : (i + 1) * small_rows], (qv_bias.shape, rel_table.shape, fc1_bias.shape))
        for i in range(gy_size)
    ]
    qkv_flat = whole_matrix(qkv_weight.reshape(qkv_weight.shape[0], -1), 3, False)
    proj_cols = whole_matrix(proj_weight.T, 1, True)
    fc1_rows = whole_matrix(fc1_weight, 1, True)
    fc2_cols = whole_matrix(fc2_weight.T, 1, False)
    qv_bias = jnp.concatenate([part[0] for part in parts], 1)
    rel_table = jnp.concatenate([part[1] for part in parts], 1)
    fc1_bias = jnp.concatenate([part[2] for part in parts], 0)
    gain_one = ln1_gain.astype(jnp.float32)
    gain_two = ln2_gain.astype(jnp.float32)
    resid = block_input.astype(jnp.float32)
    normed_one, scale_one, pre_one = layer_norm(resid, gain_one, ln1_bias.astype(jnp.float32))
    hidden_one = (pre_one.astype(jnp.bfloat16))
    bias_row = jnp.stack([qv_bias[0], jnp.zeros_like(qv_bias[0]), qv_bias[1]]).reshape(1, 3 * width)
    mixed = (matmul(hidden_one, qkv_flat) + bias_row.astype(jnp.float32)).astype(jnp.bfloat16)
    tables = attention_tables(rel_table, tok_local // IMAGE)
    context, windows, probs = attend_forward(mixed, tables)
    resid_one = resid + (matmul_nt(context, proj_cols)) + proj_bias.astype(jnp.float32)
    normed_two, scale_two, pre_two = layer_norm(resid_one, gain_two, ln2_bias.astype(jnp.float32))
    hidden_two = (pre_two.astype(jnp.bfloat16))
    pre_act = matmul(hidden_two, fc1_rows) + fc1_bias.astype(jnp.float32)
    act_full, slope = gelu_parts(pre_act)
    act_low = act_full.astype(jnp.bfloat16)
    output = (
        resid_one + (matmul_nt(act_low, fc2_cols)) + fc2_bias.astype(jnp.float32)
    ).astype(jnp.bfloat16)
    live_rows = local_live(tok_local, live_images)
    grad_out = jnp.where(live_rows[:, None], cotangent, jnp.zeros_like(cotangent))
    grad_float = grad_out.astype(jnp.float32)
    grad_full = (grad_out)
    d_fc2_bias = jnp.sum(grad_float, 0)
    d_fc2_weight = matmul_tn(grad_full, act_low)
    d_pre = matmul(grad_full, fc2_cols) * slope
    d_fc1_bias = jnp.sum(d_pre, 0)
    d_pre_low = d_pre.astype(jnp.bfloat16)
    d_fc1_weight = matmul_tn(hidden_two, d_pre_low)
    d_hidden_two = (matmul_nt(d_pre_low, fc1_rows))
    d_ln2_gain = jnp.sum(d_hidden_two * normed_two, 0)
    d_ln2_bias = jnp.sum(d_hidden_two, 0)
    d_resid_one = grad_float + norm_back(d_hidden_two, normed_two, scale_two, gain_two)
    d_proj_bias = jnp.sum(d_resid_one, 0)
    d_resid_full = (d_resid_one.astype(jnp.bfloat16))
    d_proj_weight = matmul_tn(d_resid_full, context)
    d_context = matmul(d_resid_full, proj_cols).astype(jnp.bfloat16)
    d_mixed, d_qv_bias, d_table = attend_backward(d_context, windows, probs, tables)
    d_qkv_weight = matmul_tn(hidden_one, d_mixed)
    d_hidden_one = (matmul_nt(d_mixed, qkv_flat))
    d_ln1_gain = jnp.sum(d_hidden_one * normed_one, 0)
    d_ln1_bias = jnp.sum(d_hidden_one, 0)
    d_input = (d_resid_one + norm_back(d_hidden_one, normed_one, scale_one, gain_one)).astype(
        jnp.bfloat16
    )
    d_fc2_weight = share_matrix(d_fc2_weight, 1, False).T
    d_fc1_weight = share_matrix(d_fc1_weight, 1, True)
    d_proj_weight = share_matrix(d_proj_weight, 1, True).T
    d_qkv_weight = share_matrix(d_qkv_weight, 3, False).reshape(qkv_weight.shape)
    own = (d_ln1_gain, d_ln1_bias, d_proj_bias, d_ln2_gain, d_ln2_bias, d_fc2_bias, d_qv_bias, d_table, d_fc1_bias)
    sums = unpack(sum_all(pack(own)), [value.shape for value in own])
    norm_sums = sums[:6]
    head_sums = (own_columns(sums[6], 1), own_columns(sums[7], 1), own_columns(sums[8], 0))
    return (
        output,
        d_input,
        norm_sums[0],
        norm_sums[1],
        d_qkv_weight,
        head_sums[0],
        head_sums[1],
        d_proj_weight,
        norm_sums[2],
        norm_sums[3],
        norm_sums[4],
        d_fc1_weight,
        head_sums[2],
        d_fc2_weight,
        norm_sums[5],
    )


def shards(
    block_input,
    cotangent,
    live_images,
    ln1_gain,
    ln1_bias,
    qkv_weight,
    qv_bias,
    rel_table,
    proj_weight,
    proj_bias,
    ln2_gain,
    ln2_bias,
    fc1_weight,
    fc1_bias,
    fc2_weight,
    fc2_bias,
):
    params = (
        ln1_gain,
        ln1_bias,
        qkv_weight,
        qv_bias,
        rel_table,
        proj_weight,
        proj_bias,
        ln2_gain,
        ln2_bias,
        fc1_weight,
        fc1_bias,
        fc2_weight,
        fc2_bias,
    )
    results = blocked_layer(block_input, cotangent, live_images, params)
    return results


def solution(mesh):
    return jax.shard_map(
        shards,
        mesh=mesh,
        in_specs=(
            P(("gx", "gy"), None),
            P(("gx", "gy"), None),
            P("gx"),
            P(),
            P(),
            P("gx", None, "gy"),
            P(None, "gy"),
            P(None, "gy"),
            P("gy", "gx"),
            P(),
            P(),
            P(),
            P("gx", "gy"),
            P("gy"),
            P("gy", "gx"),
            P(),
        ),
        out_specs=(
            P(("gx", "gy"), None),
            P(("gx", "gy"), None),
            P(),
            P(),
            P("gx", None, "gy"),
            P(None, "gy"),
            P(None, "gy"),
            P("gy", "gx"),
            P(),
            P(),
            P(),
            P("gx", "gy"),
            P("gy"),
            P("gy", "gx"),
            P(),
        ),
        check_vma=False,
    )
```

```python
import jax
import jax.numpy as jnp
from jax import lax
import numpy as np
from jax.experimental import pallas as pl
from jax.experimental.pallas import tpu as pltpu
from jax.sharding import PartitionSpec as P

HD = 32
GRID = 14
WIN = 7
SHIFT = 3
RELS = 169


eps_norm = 1e-05
mask_value = -100.0
inv_root_two = 0.7071067811865476
inv_root_two_pi = 0.3989422804014327


def matmul(left, right):
    return jnp.dot(left, right, preferred_element_type=jnp.float32)


def matmul_tn(left, right):
    return lax.dot_general(
        left, right, (((0,), (0,)), ((), ())), preferred_element_type=jnp.float32
    )


def matmul_nt(left, right):
    return lax.dot_general(
        left, right, (((1,), (1,)), ((), ())), preferred_element_type=jnp.float32
    )


SLOT = 64
PACK = 8
WIN_COUNT = (GRID // WIN) ** 2
IMAGE = GRID * GRID
ALIGN = 16
STEP = IMAGE // ALIGN * ALIGN
SPAN = STEP + ALIGN
far_below = -1e30


def static_tables(image_count):
    rows = np.arange(WIN_COUNT * SLOT)
    win, place = rows // SLOT, rows % SLOT
    row = (win // (GRID // WIN) * WIN + place // WIN + SHIFT) % GRID
    col = (win % (GRID // WIN) * WIN + place % WIN + SHIFT) % GRID
    token = np.where(place < WIN * WIN, row * GRID + col, -1)
    offset = np.arange(image_count) * (IMAGE - STEP)
    column = np.where(token[None] >= 0, token[None] + offset[:, None], -1)
    places = np.arange(SLOT)
    live = places < WIN * WIN
    pr, pc = places // WIN, places % WIN
    rel = (pr[None, :] - pr[:, None] + WIN - 1) * (2 * WIN - 1) + pc[None, :] - pc[:, None] + WIN - 1
    rel = np.where(live[:, None] & live[None, :], rel, -1)
    cells = np.arange(GRID)
    region = np.where(cells < GRID - WIN, 0, np.where(cells < GRID - SHIFT, 1, 2))
    shifted_row = (win // (GRID // WIN) * WIN + np.minimum(place // WIN, WIN - 1)).reshape(WIN_COUNT, SLOT)
    shifted_col = (win % (GRID // WIN) * WIN + place % WIN).reshape(WIN_COUNT, SLOT)
    ids = region[shifted_row] * 3 + region[shifted_col]
    mask = np.where(ids[:, :, None] == ids[:, None, :], 0.0, mask_value)
    mask = np.where(live[None, None, :] & live[None, :, None], mask, 0.0)
    mask = np.where(live[None, :, None], mask, far_below)
    return column.astype(np.int32), rel.astype(np.int32), mask.astype(np.float32)


def attention_tables(rel_table, image_count):
    column, rel, mask = static_tables(image_count)
    column = jnp.asarray(column)
    spots = jnp.arange(SPAN, dtype=jnp.int32)
    perm = (column[:, :, None] == spots).astype(jnp.bfloat16)
    perm_t = (column[:, None, :] == spots[:, None]).astype(jnp.bfloat16)
    heads = rel_table.shape[1]
    onehot = (jnp.arange(RELS, dtype=jnp.int32)[:, None] == jnp.asarray(rel.reshape(1, -1))).astype(
        jnp.bfloat16
    )
    bias = lax.dot_general(
        rel_table, onehot, (((0,), (0,)), ((), ())), preferred_element_type=jnp.float32
    )
    bias = bias.reshape(heads // PACK, PACK, SLOT, SLOT).transpose(0, 2, 1, 3)
    bias = bias[None] + jnp.asarray(mask)[:, None, :, None, :]
    bias = bias.reshape(WIN_COUNT, heads // PACK, SLOT, PACK * SLOT)
    owner = np.arange(PACK * SLOT)[:, None] // SLOT == np.arange(PACK * HD)[None, :] // HD
    owner = jnp.asarray(owner.astype(np.float32)).astype(jnp.bfloat16)
    return perm, perm_t, bias, owner, onehot


def spread(rows, owner):
    return jnp.concatenate([rows] * PACK, axis=0) * owner


def gather_heads(full):
    lanes = lax.broadcasted_iota(jnp.int32, (SLOT, PACK * HD), 1) // HD
    total = full[:SLOT]
    for h in range(1, PACK):
        total = jnp.where(lanes == h, full[h * SLOT : (h + 1) * SLOT], total)
    return total


def forward_kernel(qkv_ref, perm_ref, perm_t_ref, bias_ref, owner_ref, context_ref, windows_ref, probs_ref, ctx_ref):
    image = pl.program_id(0)
    width = context_ref.shape[1]
    groups = width // (PACK * HD)
    start = pl.multiple_of(image * STEP, ALIGN)
    windows_ref[0] = matmul(perm_ref[0], qkv_ref[pl.ds(start, SPAN), :]).astype(jnp.bfloat16)
    for w in range(WIN_COUNT):
        rows = slice(w * SLOT, (w + 1) * SLOT)
        for g in range(groups):
            low = g * PACK * HD
            query = windows_ref[0, rows, low : low + PACK * HD]
            keys = windows_ref[0, rows, width + low : width + low + PACK * HD]
            values = windows_ref[0, rows, 2 * width + low : 2 * width + low + PACK * HD]
            scores = matmul_nt(keys, spread(query, owner_ref[...])) * HD ** (-0.5) + bias_ref[w, g]
            raised = jnp.exp(scores - jnp.max(scores, 0, keepdims=True))
            probs = raised * (1.0 / jnp.sum(raised, 0, keepdims=True))
            probs_ref[0, w * groups + g] = probs
            full = matmul_tn(probs.astype(jnp.bfloat16), values)
            ctx_ref[rows, low : low + PACK * HD] = gather_heads(full).astype(jnp.bfloat16)

    @pl.when(image == 0)
    def _():
        context_ref[...] = jnp.zeros_like(context_ref)

    context_ref[pl.ds(start, SPAN), :] += matmul(perm_t_ref[0], ctx_ref[...]).astype(jnp.bfloat16)


def backward_kernel(
    d_context_ref, windows_ref, probs_ref, perm_ref, perm_t_ref, owner_ref,
    d_mixed_ref, d_bias_ref, d_qv_ref, d_ctx_ref, d_win_ref,
):
    image = pl.program_id(0)
    width = d_context_ref.shape[1]
    groups = width // (PACK * HD)
    start = pl.multiple_of(image * STEP, ALIGN)

    @pl.when(image == 0)
    def _():
        d_mixed_ref[...] = jnp.zeros_like(d_mixed_ref)
        d_bias_ref[...] = jnp.zeros_like(d_bias_ref)
        d_qv_ref[...] = jnp.zeros_like(d_qv_ref)

    d_ctx_ref[...] = matmul(perm_ref[0], d_context_ref[pl.ds(start, SPAN), :]).astype(jnp.bfloat16)
    for g in range(groups):
        low = g * PACK * HD
        cols = slice(low, low + PACK * HD)
        d_bias = jnp.zeros((SLOT, PACK * SLOT), jnp.float32)
        d_query_sum = jnp.zeros((1, PACK * HD), jnp.float32)
        d_value_sum = jnp.zeros((1, PACK * HD), jnp.float32)
        for w in range(WIN_COUNT):
            rows = slice(w * SLOT, (w + 1) * SLOT)
            query = windows_ref[0, rows, low : low + PACK * HD]
            keys = windows_ref[0, rows, width + low : width + low + PACK * HD]
            values = windows_ref[0, rows, 2 * width + low : 2 * width + low + PACK * HD]
            probs = probs_ref[0, w * groups + g]
            d_wide = spread(d_ctx_ref[rows, cols], owner_ref[...])
            d_probs = matmul_nt(values, d_wide)
            d_values = matmul(probs.astype(jnp.bfloat16), d_wide)
            d_scores = probs * (d_probs - jnp.sum(probs * d_probs, 0, keepdims=True))
            d_bias = d_bias + d_scores
            d_low = d_scores.astype(jnp.bfloat16)
            d_keys = matmul(d_low, spread(query, owner_ref[...])) * HD ** (-0.5)
            d_query = gather_heads(matmul_tn(d_low, keys)) * HD ** (-0.5)
            d_win_ref[rows, low : low + PACK * HD] = d_query.astype(jnp.bfloat16)
            d_win_ref[rows, width + low : width + low + PACK * HD] = d_keys.astype(jnp.bfloat16)
            d_win_ref[rows, 2 * width + low : 2 * width + low + PACK * HD] = d_values.astype(jnp.bfloat16)
            d_query_sum = d_query_sum + jnp.sum(d_query, 0, keepdims=True)
            d_value_sum = d_value_sum + jnp.sum(d_values, 0, keepdims=True)
        d_bias_ref[g] += d_bias
        d_qv_ref[0:1, cols] += d_query_sum
        d_qv_ref[1:2, cols] += d_value_sum
    d_mixed_ref[pl.ds(start, SPAN), :] += matmul(perm_t_ref[0], d_win_ref[...]).astype(jnp.bfloat16)


def whole(shape):
    return pl.BlockSpec(shape, lambda n: (0,) * len(shape))


def per_image(shape):
    return pl.BlockSpec((1,) + shape, lambda n: (n,) + (0,) * len(shape))


def attend_forward(qkv, tables):
    perm, perm_t, bias, owner, _ = tables
    tok, wide = qkv.shape
    width = wide // 3
    count, spots = perm.shape[:2]
    tiles = WIN_COUNT * width // (PACK * HD)
    return pl.pallas_call(
        forward_kernel,
        grid=(count,),
        in_specs=[whole(qkv.shape), per_image((spots, SPAN)), per_image((SPAN, spots)), whole(bias.shape), whole(owner.shape)],
        out_specs=[whole((tok, width)), per_image((spots, wide)), per_image((tiles, SLOT, PACK * SLOT))],
        out_shape=[
            jax.ShapeDtypeStruct((tok, width), jnp.bfloat16),
            jax.ShapeDtypeStruct((count, spots, wide), jnp.bfloat16),
            jax.ShapeDtypeStruct((count, tiles, SLOT, PACK * SLOT), jnp.float32),
        ],
        scratch_shapes=[pltpu.VMEM((spots, width), jnp.bfloat16)],
        cost_estimate=pl.CostEstimate(flops=6_000_000_000, bytes_accessed=24_000_000, transcendentals=tok * width * 2),
        name="attend_forward",
    )(qkv, perm, perm_t, bias, owner)


def attend_backward(d_context, windows, probs, tables):
    perm, perm_t, _, owner, onehot = tables
    tok, width = d_context.shape
    count, spots, wide = windows.shape
    groups = width // (PACK * HD)
    tiles = probs.shape[1]
    d_mixed, d_bias, d_qv = pl.pallas_call(
        backward_kernel,
        grid=(count,),
        in_specs=[
            whole(d_context.shape), per_image((spots, wide)), per_image((tiles, SLOT, PACK * SLOT)),
            per_image((spots, SPAN)), per_image((SPAN, spots)), whole(owner.shape),
        ],
        out_specs=[whole((tok, wide)), whole((groups, SLOT, PACK * SLOT)), whole((2, width))],
        out_shape=[
            jax.ShapeDtypeStruct((tok, wide), jnp.bfloat16),
            jax.ShapeDtypeStruct((groups, SLOT, PACK * SLOT), jnp.float32),
            jax.ShapeDtypeStruct((2, width), jnp.float32),
        ],
        scratch_shapes=[pltpu.VMEM((spots, width), jnp.bfloat16), pltpu.VMEM((spots, wide), jnp.bfloat16)],
        cost_estimate=pl.CostEstimate(flops=9_000_000_000, bytes_accessed=32_000_000, transcendentals=0),
        name="attend_backward",
    )(d_context, windows, probs, perm, perm_t, owner)
    d_bias = d_bias.reshape(groups, SLOT, PACK, SLOT).transpose(0, 2, 1, 3).reshape(groups * PACK, SLOT * SLOT)
    d_table = lax.dot_general(
        onehot.astype(jnp.float32), d_bias, (((1,), (1,)), ((), ())), precision=lax.Precision.HIGHEST
    )
    return d_mixed, d_qv, d_table


def gelu_parts(pre_act):
    cdf_part = 0.5 * (1.0 + jax.scipy.special.erf(pre_act * inv_root_two))
    return (
        pre_act * cdf_part,
        cdf_part + pre_act * jnp.exp(-0.5 * pre_act * pre_act) * inv_root_two_pi,
    )


def layer_norm(rows, gain, shift):
    row_mean = jnp.mean(rows, -1, keepdims=True)
    row_var = jnp.mean(rows * rows, -1, keepdims=True) - row_mean * row_mean
    inv_std = lax.rsqrt(row_var + eps_norm)
    normed = (rows - row_mean) * inv_std
    return (normed, inv_std, normed * gain + shift)


def norm_back(d_out, normed, inv_std, gain):
    d_normed = d_out * gain
    return inv_std * (
        d_normed
        - jnp.mean(d_normed, -1, keepdims=True)
        - normed * jnp.mean(d_normed * normed, -1, keepdims=True)
    )


def axis_bits(name):
    return lax.axis_size(name).bit_length() - 1


def exchange(value, name, bit):
    pairs = [(i, i ^ (1 << bit)) for i in range(lax.axis_size(name))]
    return lax.ppermute(value, name, pairs)


def own_bit(name, bit):
    return (lax.axis_index(name) >> bit) & 1


def gather_order(name, flip):
    bits = list(range(axis_bits(name)))[::-1]
    if flip and len(bits) > 2:
        bits = [bits[1], bits[0]] + bits[2:]
    return bits


def gather_axis(block, name, flip=False):
    rows, columns = block.shape
    done = []
    for bit in gather_order(name, flip):
        higher = 1 << len([b for b in done if b > bit])
        lower = 1 << len([b for b in done if b < bit])
        mine = block.reshape(higher, 1, lower * rows, columns)
        theirs = exchange(block, name, bit).reshape(mine.shape)
        upper = own_bit(name, bit) == 1
        block = jnp.concatenate(
            [jnp.where(upper, theirs, mine), jnp.where(upper, mine, theirs)], axis=1
        ).reshape(higher * 2 * lower * rows, columns)
        done.append(bit)
    return block


def scatter_axis(totals, name, flip=False):
    rows = totals[0].shape[0] // lax.axis_size(name)
    widths = [total.shape[1] for total in totals]
    starts = [sum(widths[:k]) for k in range(len(widths))]
    order = gather_order(name, flip)[::-1]
    for place, bit in enumerate(order):
        left = order[place + 1 :]
        higher = 1 << len([b for b in left if b > bit])
        lower = 1 << len([b for b in left if b < bit])
        upper = own_bit(name, bit) == 1
        kept, away = [], []
        for total, columns in zip(totals, widths):
            view = total.reshape(higher, 2, lower * rows, columns)
            first, second = view[:, 0], view[:, 1]
            kept.append(jnp.where(upper, second, first).reshape(-1, columns))
            away.append(jnp.where(upper, first, second).astype(jnp.bfloat16).reshape(-1, columns))
        came = exchange(jnp.concatenate(away, 1), name, bit)
        totals = [
            part + came[:, at : at + columns].astype(jnp.float32)
            for part, at, columns in zip(kept, starts, widths)
        ]
    return totals


def sum_all(value):
    for name in ("gx", "gy"):
        for bit in range(axis_bits(name)):
            came = exchange(value, name, bit)
            value = value + came
    return value


def join_columns(blocks, groups):
    gy_size, rows, wide = blocks.shape
    blocks = blocks.reshape(gy_size, rows, groups, wide // groups)
    return blocks.transpose(1, 2, 0, 3).reshape(rows, groups * gy_size * (wide // groups))


def split_columns(rows_block, groups):
    gy_size = lax.axis_size("gy")
    rows, wide = rows_block.shape
    columns = wide // groups // gy_size
    blocks = rows_block.reshape(rows, groups, gy_size, columns).transpose(2, 0, 1, 3)
    return blocks.reshape(gy_size * rows, groups * columns)


def pack(values, lanes):
    flat = [value.reshape(-1) for value in values]
    size = sum(value.shape[0] for value in flat)
    return jnp.pad(jnp.concatenate(flat), (0, -size % (16 * lanes))).reshape(-1, lanes)


def unpack(packed, shapes):
    flat, at, out = packed.reshape(-1), 0, []
    for shape in shapes:
        size = int(np.prod(shape))
        out.append(flat[at : at + size].reshape(shape))
        at += size
    return out


def own_columns(summed, axis):
    size = summed.shape[axis] // lax.axis_size("gy")
    return lax.dynamic_slice_in_dim(summed, lax.axis_index("gy") * size, size, axis)


def local_live(tok_local, live_images):
    position = lax.axis_index("gy")
    per_device = tok_local // (GRID * GRID)
    slot_index = position * per_device + jnp.arange(tok_local, dtype=jnp.int32) // (GRID * GRID)
    return slot_index < live_images[0]


def blocked_layer(block_input, cotangent, live_images, params):
    (
        ln1_gain,
        ln1_bias,
        qkv_weight,
        qv_bias,
        rel_table,
        proj_weight,
        proj_bias,
        ln2_gain,
        ln2_bias,
        fc1_weight,
        fc1_bias,
        fc2_weight,
        fc2_bias,
    ) = params
    tok_local, width = block_input.shape
    gy_size = lax.axis_size("gy")
    block_rows = qkv_weight.shape[0]
    first = jnp.concatenate([qkv_weight.reshape(block_rows, -1), proj_weight.T], 1)
    small = pack((qv_bias, rel_table, fc1_bias), first.shape[1])
    first = gather_axis(jnp.concatenate([first, small], 0), "gy")
    first = first.reshape(gy_size, -1, first.shape[1])
    parts = [
        unpack(first[i, block_rows:], (qv_bias.shape, rel_table.shape, fc1_bias.shape))
        for i in range(gy_size)
    ]
    qkv_wide = 3 * qkv_weight.shape[2]
    first = jnp.concatenate(
        [join_columns(first[:, :block_rows, :qkv_wide], 3), join_columns(first[:, :block_rows, qkv_wide:], 1)], 1
    )
    first = gather_axis(first, "gx")
    later = gather_axis(jnp.concatenate([fc1_weight, fc2_weight.T], 1), "gy")
    first, later = lax.optimization_barrier((first, later))
    qkv_flat, proj_cols = first[:, : 3 * width], first[:, 3 * width :]
    later = later.reshape(gy_size, block_rows, -1)
    hidden_local = fc1_weight.shape[1]
    fc1_rows = gather_axis(join_columns(later[:, :, :hidden_local], 1), "gx", True)
    fc2_cols = gather_axis(join_columns(later[:, :, hidden_local:], 1), "gx")
    qv_bias = jnp.concatenate([part[0] for part in parts], 1)
    rel_table = jnp.concatenate([part[1] for part in parts], 1)
    fc1_bias = jnp.concatenate([part[2] for part in parts], 0)
    gain_one = ln1_gain.astype(jnp.float32)
    gain_two = ln2_gain.astype(jnp.float32)
    resid = block_input.astype(jnp.float32)
    normed_one, scale_one, pre_one = layer_norm(resid, gain_one, ln1_bias.astype(jnp.float32))
    hidden_one = (pre_one.astype(jnp.bfloat16))
    bias_row = jnp.stack([qv_bias[0], jnp.zeros_like(qv_bias[0]), qv_bias[1]]).reshape(1, 3 * width)
    mixed = (matmul(hidden_one, qkv_flat) + bias_row.astype(jnp.float32)).astype(jnp.bfloat16)
    tables = attention_tables(rel_table, tok_local // IMAGE)
    context, windows, probs = attend_forward(mixed, tables)
    resid_one = resid + (matmul_nt(context, proj_cols)) + proj_bias.astype(jnp.float32)
    normed_two, scale_two, pre_two = layer_norm(resid_one, gain_two, ln2_bias.astype(jnp.float32))
    hidden_two = (pre_two.astype(jnp.bfloat16))
    pre_act = matmul(hidden_two, fc1_rows) + fc1_bias.astype(jnp.float32)
    act_full, slope = gelu_parts(pre_act)
    act_low = act_full.astype(jnp.bfloat16)
    output = (
        resid_one + (matmul_nt(act_low, fc2_cols)) + fc2_bias.astype(jnp.float32)
    ).astype(jnp.bfloat16)
    live_rows = local_live(tok_local, live_images)
    grad_out = jnp.where(live_rows[:, None], cotangent, jnp.zeros_like(cotangent))
    grad_float = grad_out.astype(jnp.float32)
    grad_full = (grad_out)
    d_fc2_bias = jnp.sum(grad_float, 0)
    d_fc2_weight = matmul_tn(grad_full, act_low)
    d_pre = matmul(grad_full, fc2_cols) * slope
    d_fc1_bias = jnp.sum(d_pre, 0)
    d_pre_low = d_pre.astype(jnp.bfloat16)
    d_fc1_weight = matmul_tn(hidden_two, d_pre_low)
    d_hidden_two = (matmul_nt(d_pre_low, fc1_rows))
    d_ln2_gain = jnp.sum(d_hidden_two * normed_two, 0)
    d_ln2_bias = jnp.sum(d_hidden_two, 0)
    d_resid_one = grad_float + norm_back(d_hidden_two, normed_two, scale_two, gain_two)
    d_proj_bias = jnp.sum(d_resid_one, 0)
    d_resid_full = (d_resid_one.astype(jnp.bfloat16))
    d_proj_weight = matmul_tn(d_resid_full, context)
    d_context = matmul(d_resid_full, proj_cols).astype(jnp.bfloat16)
    d_context, d_fc1_weight, d_fc2_weight = lax.optimization_barrier((d_context, d_fc1_weight, d_fc2_weight))
    (d_fc1_part,) = scatter_axis([d_fc1_weight], "gx", True)
    (d_fc2_part,) = scatter_axis([d_fc2_weight], "gx", False)
    (early,) = scatter_axis([jnp.concatenate([split_columns(d_fc1_part, 1), split_columns(d_fc2_part, 1)], 1)], "gy")
    d_fc1_weight, d_fc2_weight = early[:, :hidden_local], early[:, hidden_local:].T
    d_mixed, d_qv_bias, d_table = attend_backward(d_context, windows, probs, tables)
    d_qkv_weight = matmul_tn(hidden_one, d_mixed)
    d_hidden_one = (matmul_nt(d_mixed, qkv_flat))
    d_ln1_gain = jnp.sum(d_hidden_one * normed_one, 0)
    d_ln1_bias = jnp.sum(d_hidden_one, 0)
    d_input = (d_resid_one + norm_back(d_hidden_one, normed_one, scale_one, gain_one)).astype(
        jnp.bfloat16
    )
    late_parts = scatter_axis([d_qkv_weight, d_proj_weight], "gx", False)
    late_parts = [split_columns(part, count) for part, count in zip(late_parts, (3, 1))]
    (late,) = scatter_axis([jnp.concatenate(late_parts, 1)], "gy", False)
    d_qkv_weight = late[:, :qkv_wide].reshape(qkv_weight.shape)
    d_proj_weight = late[:, qkv_wide:].T
    own = (d_ln1_gain, d_ln1_bias, d_proj_bias, d_ln2_gain, d_ln2_bias, d_fc2_bias, d_qv_bias, d_table, d_fc1_bias)
    sums = unpack(sum_all(pack(own, 128)), [value.shape for value in own])
    norm_sums = sums[:6]
    head_sums = (own_columns(sums[6], 1), own_columns(sums[7], 1), own_columns(sums[8], 0))
    return (
        output,
        d_input,
        norm_sums[0],
        norm_sums[1],
        d_qkv_weight,
        head_sums[0],
        head_sums[1],
        d_proj_weight,
        norm_sums[2],
        norm_sums[3],
        norm_sums[4],
        d_fc1_weight,
        head_sums[2],
        d_fc2_weight,
        norm_sums[5],
    )


def shards(
    block_input,
    cotangent,
    live_images,
    ln1_gain,
    ln1_bias,
    qkv_weight,
    qv_bias,
    rel_table,
    proj_weight,
    proj_bias,
    ln2_gain,
    ln2_bias,
    fc1_weight,
    fc1_bias,
    fc2_weight,
    fc2_bias,
):
    params = (
        ln1_gain,
        ln1_bias,
        qkv_weight,
        qv_bias,
        rel_table,
        proj_weight,
        proj_bias,
        ln2_gain,
        ln2_bias,
        fc1_weight,
        fc1_bias,
        fc2_weight,
        fc2_bias,
    )
    return blocked_layer(block_input, cotangent, live_images, params)


def solution(mesh):
    return jax.shard_map(
        shards,
        mesh=mesh,
        in_specs=(
            P(("gx", "gy"), None),
            P(("gx", "gy"), None),
            P("gx"),
            P(),
            P(),
            P("gx", None, "gy"),
            P(None, "gy"),
            P(None, "gy"),
            P("gy", "gx"),
            P(),
            P(),
            P(),
            P("gx", "gy"),
            P("gy"),
            P("gy", "gx"),
            P(),
        ),
        out_specs=(
            P(("gx", "gy"), None),
            P(("gx", "gy"), None),
            P(),
            P(),
            P("gx", None, "gy"),
            P(None, "gy"),
            P(None, "gy"),
            P("gy", "gx"),
            P(),
            P(),
            P(),
            P("gx", "gy"),
            P("gy"),
            P("gy", "gx"),
            P(),
        ),
        check_vma=False,
    )
```
